32 devices in a mesh: groups: 2 (over y), leaf: 4 (over z), cols: 2 (over x), sub: 2 (over core).
Axes of the slice: x: 2, y: 2, z: 4, core: 2. Of those that a mesh axis runs over, the one named last changes fastest.
Arguments:
- right_side: float32 [512, 4, 768], P(('groups', 'cols'), 'leaf', 'sub'), parts along dimension 0, may hold values from -12 to 12
- leaf_diag: float32 [8, 768, 768], P(('groups', 'leaf'), 'sub'), parts along dimension 0, as said below
- leaf_rot: float32 [8, 768, 768], P(('groups', 'leaf'), 'sub'), parts along dimension 0, as said below
- node_rot: float32 [8, 768, 768], P(('groups', 'leaf'), 'sub'), parts along dimension 0, as said below
- coupling: float32 [8, 384, 384], P(('groups', 'leaf')), parts along dimension 0, may hold values from -0.15 to 0.15, as said below
- child_order: int32 [8], P(('groups', 'leaf')), parts along dimension 0, may hold values 0 or 1
Outputs:
- solution: float32 [512, 4, 768], P(('groups', 'cols'), 'leaf', 'sub'), parts along dimension 0
The draws below stay inside these ranges and needn't reach their ends.
There are 2 independent parts, one for each index of `groups`. The reference program is written for one: setup_inputs(seed, part) draws one part's arguments, and reference() takes and returns one part's arrays. A program takes and returns all parts, laid end to end along the dimension named above; each array names one. Nothing has to cross between parts.
Inputs may be any that keep to these rules, and one draw needn't show every extreme that they name: `child_order`: entry g with 0 < g < 4 orders the children of the node at gap g; entry 0 belongs to no node. `leaf_diag`: every block is symmetric, with smallest eigenvalue at least 3. `leaf_rot`: every block is orthogonal up to rounding. `node_rot`: every block is orthogonal up to rounding; entry 0 belongs to no node. `coupling`: entry 0 belongs to no node.
All inputs are finite; a program needn't handle non-finite values. No bound on the sum of `child_order` on one device may be relied on, other than what follows from the above.
Results may differ from the reference program's by a relative error of at most 0.00013.
Values sent between devices are 32-bit elements; how exact they have to be, the bound alone decides.
A program may use at most 128 MiB of HBM per device.

```python
import math
import jax
import jax.numpy as jnp
from jax import lax

LEAF_ORDER = 768
NODE_RANK = 384
LEAVES = 4
LEVELS = 2
NRHS = 256


def spd_blocks(seed_key):
    noise_key = jax.random.fold_in(seed_key, 0)
    noise = jax.random.normal(noise_key, (LEAVES, LEAF_ORDER, LEAF_ORDER), jnp.float32)
    gram_part = jnp.einsum('lij,lkj->lik', noise, noise) / LEAF_ORDER
    gram_part = 0.5 * (gram_part + jnp.swapaxes(gram_part, 1, 2))
    return 3.0 * jnp.eye(LEAF_ORDER, dtype=jnp.float32) + gram_part


def orthogonal_blocks(seed_key):
    raw_blocks = jax.random.normal(seed_key, (LEAVES, LEAF_ORDER, LEAF_ORDER), jnp.float32)
    orthogonal, upper_part = jnp.linalg.qr(raw_blocks)
    return orthogonal


def draw_leaf_diag(key, part):
    return spd_blocks(jax.random.fold_in(key, 101))


def draw_leaf_rot(key, part):
    return orthogonal_blocks(jax.random.fold_in(key, 202))


def draw_node_rot(key, part):
    return orthogonal_blocks(jax.random.fold_in(key, 303))


def draw_coupling(key, part):
    coupling_key = jax.random.fold_in(key, 404)
    spread = 1.0 / math.sqrt(2.0 * NODE_RANK)
    block_shape = (LEAVES, NODE_RANK, NODE_RANK)
    values = jax.random.normal(coupling_key, block_shape, jnp.float32)
    return jnp.clip(values * spread, -0.15, 0.15)


def place_ends(values, key, least, high):
    place = [jax.random.randint(jax.random.fold_in(key, axis), (), 0, length) for axis, length in enumerate(values.shape)]
    widest = values.shape.index(max(values.shape))
    beside = place[:widest] + [(place[widest] + 1) % values.shape[widest]] + place[widest + 1:]
    return values.at[tuple(place)].set(least).at[tuple(beside)].set(high)


def block_levels(rng, dims, pieces, low, high):
    level = 1.0
    for position, parts in pieces:
        draws = jax.random.uniform(jax.random.fold_in(jax.random.fold_in(rng, 6), position), (parts,), jnp.float32, low / len(pieces), high / len(pieces))
        level = level * jnp.repeat(jnp.exp(draws), dims[position] // parts).reshape((-1,) + (1,) * (len(dims) - 1 - position))
    return level


def bell_draw(rng, extent, width, most, cuts=(), kind=jnp.bfloat16):
    entries = jax.random.normal(rng, extent, jnp.float32) * width
    if len(cuts) > 0:
        entries = block_levels(rng, extent, cuts, -0.22, 0.18) * entries
    return jnp.clip(entries, min=-most, max=most).astype(kind)


def setup_inputs(seed: int = 0, part: int = 0) -> dict:
    arg_keys = jax.random.split(jax.random.key(seed), 7)
    part_splits = jax.random.split(jax.random.fold_in(arg_keys[6], part), 7)
    return {
        "right_side": bell_draw(part_splits[0], (NRHS, LEAVES, LEAF_ORDER), 3.0, 12.0, ((0, 2), (1, 4), (2, 2)), jnp.float32),
        "leaf_diag": draw_leaf_diag(jax.random.fold_in(jax.random.fold_in(arg_keys[6], part), 71), part),
        "leaf_rot": draw_leaf_rot(jax.random.fold_in(jax.random.fold_in(arg_keys[6], part), 71), part),
        "node_rot": draw_node_rot(jax.random.fold_in(jax.random.fold_in(arg_keys[6], part), 71), part),
        "coupling": draw_coupling(jax.random.fold_in(jax.random.fold_in(arg_keys[6], part), 71), part),
        "child_order": place_ends((jax.random.randint(part_splits[5], (LEAVES,), 0, 2) < 1).astype(jnp.int32), jax.random.fold_in(part_splits[5], 1), 0, 1),
    }


highest = lax.Precision.HIGHEST

def matrix_product(left_mat, right_mat):
    return jnp.dot(left_mat.astype(jnp.float32), right_mat.astype(jnp.float32), preferred_element_type=jnp.float32, precision=highest)

def lower_triangle_solve(factor, values):
    return lax.linalg.triangular_solve(factor, values, left_side=True, lower=True)

def upper_triangle_solve(factor, values):
    return lax.linalg.triangular_solve(factor, values, left_side=True, lower=True, transpose_a=True)

def eliminate(combined_block, rotation_matrix, right_hand_columns):
    eliminated_count = LEAF_ORDER - NODE_RANK
    rotation_eliminated = rotation_matrix[:, :eliminated_count]
    rotation_retained = rotation_matrix[:, eliminated_count:]
    product_eliminated = matrix_product(combined_block, rotation_eliminated)
    eliminated_block = matrix_product(rotation_eliminated.T, product_eliminated)
    crossing_block = matrix_product(product_eliminated.T, rotation_retained)
    prod_kept = matrix_product(combined_block, rotation_retained)
    kept_block = matrix_product(rotation_retained.T, prod_kept)
    cholesky_lower = jnp.linalg.cholesky(eliminated_block)
    coupled = lower_triangle_solve(cholesky_lower, crossing_block)
    complement_block = kept_block - matrix_product(coupled.T, coupled)
    right_hand_eliminated = matrix_product(right_hand_columns, rotation_eliminated)
    rhs_kept = matrix_product(right_hand_columns, rotation_retained)
    partial_answer = lower_triangle_solve(cholesky_lower, right_hand_eliminated.T)
    carried_state = rhs_kept - matrix_product(partial_answer.T, coupled)
    return ((complement_block, carried_state), (cholesky_lower, coupled, partial_answer))

def recover(factors, rotation_matrix, retained_answer):
    cholesky_lower, coupled, partial_answer = factors
    residual_vector = partial_answer - matrix_product(coupled, retained_answer.T)
    eliminated_answer = upper_triangle_solve(cholesky_lower, residual_vector)
    complete_answer = jnp.concatenate([eliminated_answer.T, retained_answer], axis=1)
    return matrix_product(complete_answer, rotation_matrix.T)

def assemble(from_left, from_right, flipped, coupling_block):
    left_schur, left_carried = from_left
    right_schur, right_carried = from_right
    first_schur = jnp.where(flipped, right_schur, left_schur)
    second_schur = jnp.where(flipped, left_schur, right_schur)
    first_carried = jnp.where(flipped, right_carried, left_carried)
    second_carried = jnp.where(flipped, left_carried, right_carried)
    upper_rows = jnp.concatenate([first_schur, coupling_block], axis=1)
    lower_rows = jnp.concatenate([coupling_block.T, second_schur], axis=1)
    combined_block = jnp.concatenate([upper_rows, lower_rows], axis=0)
    return (combined_block, jnp.concatenate([first_carried, second_carried], axis=1))

def root_solve(complement_block, carried_state):
    cholesky_lower = jnp.linalg.cholesky(complement_block)
    return upper_triangle_solve(cholesky_lower, lower_triangle_solve(cholesky_lower, carried_state.T)).T

def reference(right_side, leaf_diag, leaf_rot, node_rot, coupling, child_order):
    leaf_payload = {}
    leaf_factors = {}
    for leaf_idx in range(LEAVES):
        payload, factors = eliminate(leaf_diag[leaf_idx], leaf_rot[leaf_idx], right_side[:, leaf_idx, :])
        leaf_payload[leaf_idx] = payload
        leaf_factors[leaf_idx] = factors
    node_payload = {}
    node_factors = {}
    for level_idx in range(1, LEVELS + 1):
        node_span = 2 ** (level_idx - 1)
        for node_gap in range(node_span, LEAVES, 2 * node_span):
            if level_idx == 1:
                from_left = leaf_payload[node_gap - 1]
                from_right = leaf_payload[node_gap]
            else:
                quarter = node_span // 2
                from_left = node_payload[node_gap - quarter]
                from_right = node_payload[node_gap + quarter]
            entry = node_gap
            combined_block, rhs_merged = assemble(from_left, from_right, child_order[entry] != 0, coupling[entry])
            payload, factors = eliminate(combined_block, node_rot[entry], rhs_merged)
            node_payload[node_gap] = payload
            node_factors[node_gap] = factors
    root_gap = LEAVES // 2
    node_kept = {root_gap: root_solve(*node_payload[root_gap])}
    leaf_kept = {}
    for level_idx in range(LEVELS, 0, -1):
        node_span = 2 ** (level_idx - 1)
        for node_gap in range(node_span, LEAVES, 2 * node_span):
            entry = node_gap
            solved = recover(node_factors[node_gap], node_rot[entry], node_kept[node_gap])
            first_part = solved[:, :NODE_RANK]
            second_part = solved[:, NODE_RANK:]
            flipped = child_order[entry] != 0
            to_left = jnp.where(flipped, second_part, first_part)
            to_right = jnp.where(flipped, first_part, second_part)
            if level_idx == 1:
                leaf_kept[node_gap - 1] = to_left
                leaf_kept[node_gap] = to_right
            else:
                quarter = node_span // 2
                node_kept[node_gap - quarter] = to_left
                node_kept[node_gap + quarter] = to_right
    columns = [recover(leaf_factors[leaf_idx], leaf_rot[leaf_idx], leaf_kept[leaf_idx]) for leaf_idx in range(LEAVES)]
    return jnp.stack(columns, axis=1)
```

```python
import functools

import jax
import jax.numpy as jnp
from jax import lax
from jax.experimental import pallas as pl
from jax.experimental.pallas import tpu as pltpu
from jax.sharding import PartitionSpec as P

f32 = jnp.float32
bf16 = jnp.bfloat16

VMEM_SPEC = pl.BlockSpec(memory_space=pltpu.VMEM)
SMEM_SPEC = pl.BlockSpec(memory_space=pltpu.SMEM)
NN = (((1,), (0,)), ((), ()))
NT = (((1,), (1,)), ((), ()))


def split(x):
    high = x.astype(bf16)
    return high, (x - high.astype(f32)).astype(bf16)


def one(a, b, dims=NN):
    return lax.dot_general(a, b, dims, preferred_element_type=f32)


def product(a, b, dims=NN):
    return one(a[0], b[0], dims) + (one(a[0], b[1], dims) + one(a[1], b[0], dims))


def eye(n):
    return (
        lax.broadcasted_iota(jnp.int32, (n, n), 0) == lax.broadcasted_iota(jnp.int32, (n, n), 1)
    ).astype(f32)


def invert(e_ref, x_ref, r_ref):
    n = e_ref.shape[0]
    e = e_ref[...]
    bound = jnp.max(jnp.sum(jnp.abs(e), axis=0, keepdims=True))
    scale = 1.9 / bound
    start = eye(n) - scale * e
    x_ref[...] = scale * (eye(n) + start)
    low = start.astype(bf16)
    first = one(low, low)
    r_ref[...] = first

    def rough_go(state):
        step, size = state
        return jnp.logical_and(step < 40, size > 4e-3)

    def rough(state):
        step, _ = state
        r = r_ref[...].astype(bf16)
        x = x_ref[...]
        x_ref[...] = x + one(x.astype(bf16), r)
        squared = one(r, r)
        r_ref[...] = squared
        return step + 1, jnp.sum(squared * squared)

    lax.while_loop(rough_go, rough, (jnp.int32(0), jnp.sum(first * first)))
    e_parts = split(e_ref[...])

    def residual():
        r = eye(n) - product(e_parts, split(x_ref[...]))
        r_ref[...] = r
        return jnp.sum(r * r)

    size = residual()
    restart = jnp.logical_not(size < 0.25)

    @pl.when(restart)
    def _():
        x_ref[...] = scale * eye(n)
        residual()

    def fine_go(state):
        step, now, before = state
        stalled = jnp.logical_and(before < 1e-2, now > 0.5 * before)
        more = jnp.logical_and(now > 1e-10, jnp.logical_not(stalled))
        return jnp.logical_and(step < 64, more)

    def fine(state):
        step, now, _ = state
        x = x_ref[...]
        small = now < 4e-6
        x_ref[...] = x + product(split(x), split(r_ref[...]))
        after = lax.cond(small, lambda: jnp.float32(0.0), residual)
        return step + 1, after, now

    lax.while_loop(
        fine_go, fine, (jnp.int32(0), jnp.where(restart, jnp.float32(1e6), size), jnp.float32(1e9))
    )


def eliminate(a, q, qt, b, p, e_ref, c_ref, m_ref, r_ref):
    n = e_ref.shape[0]
    full = a[0].shape[0]
    a_parts = (a[0][...], a[1][...])
    for j in range(0, full, n):
        part = product(a_parts, (q[0][:, j : j + n], q[1][:, j : j + n]))
        p[0][:, j : j + n], p[1][:, j : j + n] = split(part)
    top = (qt[0][:n, :], qt[1][:n, :])
    e_ref[...] = product(top, (p[0][:, :n], p[1][:, :n]))
    c_ref[...] = product(top, (p[0][:, n:], p[1][:, n:]))
    invert(e_ref, m_ref, r_ref)
    kept = product((qt[0][n:, :], qt[1][n:, :]), (p[0][:, n:], p[1][:, n:]))
    c_parts = split(c_ref[...])
    g = product(split(m_ref[...]), c_parts)
    g_parts = split(g)
    ct_parts = split(c_ref[...].T)
    schur = kept - product(ct_parts, g_parts)
    bq = product(b, (q[0][...], q[1][...]))
    be = bq[:, :n]
    carried = bq[:, n:] - product(split(be), g_parts)
    return schur, carried, g, be


def load_rotation(sub, q_own, q_oth, q, qt):
    n = q_own.shape[0]
    for which, ref in ((sub, q_own), (1 - sub, q_oth)):
        rows = pl.ds(pl.multiple_of(which * n, n), n)
        high, low = split(ref[...])
        q[0][rows, :] = high
        q[1][rows, :] = low
    if qt is not None:
        qt[0][...] = q[0][...].T
        qt[1][...] = q[1][...].T


def by_half(sub, own, oth):
    first = sub == 0
    return jnp.where(first, own, oth), jnp.where(first, oth, own)


def recover(be, m, g, x, q):
    w = product(split(be), split(m)) - product(split(x), split(g), NT)
    return product(split(jnp.concatenate([w, x], axis=1)), (q[0][...], q[1][...]), NT)


def leaf_kernel(
    flags, a_own, a_oth, q_own, q_oth, b_own, b_oth,
    s_out, half_out, c_out, m_out, g_out, be_out,
    ah, al, qh, ql, qth, qtl, ph, pl_, e_ref, c_ref, r_ref,
):
    sub = flags[0]
    load_rotation(sub, a_own, a_oth, (ah, al), None)
    load_rotation(sub, q_own, q_oth, (qh, ql), (qth, qtl))
    b = jnp.concatenate(by_half(sub, b_own[...], b_oth[...]), axis=1)
    s, c, g, be = eliminate(
        (ah, al), (qh, ql), (qth, qtl), split(b), (ph, pl_), e_ref, c_ref, m_out, r_ref
    )
    s_out[...] = s
    rows = half_out.shape[0]
    half_out[...] = s_out[pl.ds(pl.multiple_of(sub * rows, rows), rows), :]
    c_out[...] = c
    g_out[...] = g
    be_out[...] = be


def node_kernel(is_root, right_whole, *refs):
    flags, l_own, l_oth = refs[:3]
    refs = refs[3:]
    if right_whole:
        (r_own,), refs = refs[:1], refs[1:]
    else:
        (r_own, r_oth), refs = refs[:2], refs[2:]
    (cl, cr, coup, q_own, q_oth), refs = refs[:5], refs[5:]
    if is_root:
        (left_out, right_out), refs = refs[:2], refs[2:]
        (x_ref, g_ref, s_ref, minv_ref), refs = refs[:4], refs[4:]
    else:
        (half_out, c_out, x_ref, g_ref, be_out), refs = refs[:5], refs[5:]
        (s_ref,), refs = refs[:1], refs[1:]
    ah, al, qh, ql, qth, qtl, ph, pl_, e_ref, c_ref, r_ref = refs
    sub = flags[0]
    n = e_ref.shape[0]

    @pl.when(flags[1] != 0)
    def _():
        load_rotation(sub, q_own, q_oth, (qh, ql), (qth, qtl))
        flipped = flags[2] != 0
        left = jnp.concatenate(by_half(sub, l_own[...], l_oth[...]), axis=0)
        if right_whole:
            right = r_own[...]
        else:
            right = jnp.concatenate(by_half(sub, r_own[...], r_oth[...]), axis=0)
        coupling = coup[...]
        for row, col, value in (
            (0, 0, jnp.where(flipped, right, left)),
            (0, n, coupling),
            (n, 0, coupling.T),
            (n, n, jnp.where(flipped, left, right)),
        ):
            high, low = split(value)
            ah[row : row + n, col : col + n] = high
            al[row : row + n, col : col + n] = low
        b = jnp.concatenate(
            [jnp.where(flipped, cr[...], cl[...]), jnp.where(flipped, cl[...], cr[...])], axis=1
        )
        s, c, g, be = eliminate(
            (ah, al), (qh, ql), (qth, qtl), split(b), (ph, pl_), e_ref, c_ref, x_ref, r_ref
        )
        s_ref[...] = s
        g_ref[...] = g
        if is_root:
            invert(s_ref, minv_ref, r_ref)
            x = product(split(c), split(minv_ref[...]))
            v = recover(be, x_ref[...], g_ref[...], x, (qh, ql))
            left_out[...] = jnp.where(flipped, v[:, n:], v[:, :n])
            right_out[...] = jnp.where(flipped, v[:, :n], v[:, n:])
        else:
            rows = half_out.shape[0]
            half_out[...] = s_ref[pl.ds(pl.multiple_of(sub * rows, rows), rows), :]
            c_out[...] = c
            be_out[...] = be


def down_kernel(flags, be, m, g, xa, xb, q_own, q_oth, left_out, right_out, qh, ql):
    sub = flags[0]
    n = m.shape[0]

    @pl.when(flags[1] != 0)
    def _():
        load_rotation(sub, q_own, q_oth, (qh, ql), None)
        x = jnp.where(flags[3] != 0, xa[...], xb[...])
        v = recover(be[...], m[...], g[...], x, (qh, ql))
        flipped = flags[2] != 0
        left_out[...] = jnp.where(flipped, v[:, n:], v[:, :n])
        right_out[...] = jnp.where(flipped, v[:, :n], v[:, n:])


def shape(*dims):
    return jax.ShapeDtypeStruct(dims, f32)


def call(kernel, outs, scratch, args, name):
    return pl.pallas_call(
        kernel,
        out_shape=outs,
        in_specs=[SMEM_SPEC] + [VMEM_SPEC] * (len(args) - 1),
        out_specs=jax.tree.map(lambda _: VMEM_SPEC, outs),
        scratch_shapes=scratch,
        compiler_params=pltpu.CompilerParams(vmem_limit_bytes=56 * 2**20),
        name=name,
    )(*args)


def swap(value):
    return lax.ppermute(value, "sub", [(0, 1), (1, 0)])


def hop(value, pairs):
    return lax.ppermute(value, "leaf", pairs)


def local(right_side, leaf_diag, leaf_rot, node_rot, coupling, child_order):
    sub = lax.axis_index("sub")
    pos = lax.axis_index("leaf")
    leaves = lax.axis_size("leaf")
    levels = leaves.bit_length() - 1
    full = leaf_diag.shape[-1]
    n = coupling.shape[-1]
    count = right_side.shape[0] // 2
    rows = n // 2

    b_all = right_side[:, 0, :]
    b_own = lax.dynamic_slice_in_dim(b_all, sub * count, count, 0)
    b_oth = swap(lax.dynamic_slice_in_dim(b_all, (1 - sub) * count, count, 0))
    q_own, a_own, r_own = leaf_rot[0], leaf_diag[0], node_rot[0]
    q_oth, a_oth, r_oth = swap(q_own), swap(a_own), swap(r_own)
    flip = child_order[0]

    def flags(active, choice):
        return jnp.stack(
            [sub.astype(jnp.int32), active.astype(jnp.int32), flip, choice.astype(jnp.int32)]
        )

    always = jnp.ones((), jnp.int32)
    big = [pltpu.VMEM((full, full), bf16)] * 8
    small = [pltpu.VMEM((n, n), f32)] * 3
    schur, half, carried, m_leaf, g_leaf, be_leaf = call(
        leaf_kernel,
        (shape(n, n), shape(rows, n), shape(count, n), shape(n, n), shape(n, n), shape(count, n)),
        big + small,
        (flags(always, always), a_own, a_oth, q_own, q_oth, b_own, b_oth),
        "leaf_up",
    )
    kept = {}
    for level in range(1, levels + 1):
        span = 2 ** (level - 1)
        gaps = range(span, leaves, 2 * span)
        owner = pos % (2 * span) == span
        step = max(span // 2, 1)
        to_right = [(g - step, g) for g in gaps]
        l_own, cl = hop(half, to_right), hop(carried, to_right)
        l_oth = swap(l_own)
        if level == 1:
            right, cr = (schur,), carried
        else:
            to_left = [(g + step, g) for g in gaps]
            got, cr = hop(half, to_left), hop(carried, to_left)
            right = (got, swap(got))
        is_root = level == levels
        args = (flags(owner, always), l_own, l_oth, *right, cl, cr, coupling[0], r_own, r_oth)
        body = functools.partial(node_kernel, is_root, level == 1)
        if is_root:
            left_x, right_x = call(
                body, (shape(count, n), shape(count, n)),
                [pltpu.VMEM((n, n), f32)] * 4 + big + small, args, "root",
            )
        else:
            half, carried, m_node, g_node, be_node = call(
                body,
                (shape(rows, n), shape(count, n), shape(n, n), shape(n, n), shape(count, n)),
                [pltpu.VMEM((n, n), f32)] + big + small, args, "node_up",
            )
            kept[level] = (be_node, m_node, g_node)
    turn = [pltpu.VMEM((full, full), bf16)] * 2
    for level in range(levels, 0, -1):
        span = 2 ** (level - 1)
        gaps = range(span, leaves, 2 * span)
        if level < levels:
            owner = pos % (2 * span) == span
            left_x, right_x = call(
                down_kernel,
                (shape(count, n), shape(count, n)),
                turn,
                (flags(owner, choice), *kept[level], got_left, got_right, r_own, r_oth),
                "node_down",
            )
        if level == 1:
            got_left = hop(left_x, [(g, g - 1) for g in gaps])
            got_right = right_x
            choice = pos % 2 == 0
        else:
            step = span // 2
            got_left = hop(left_x, [(g, g - step) for g in gaps])
            got_right = hop(right_x, [(g, g + step) for g in gaps])
            choice = pos // span % 2 == 0
    first, second = call(
        down_kernel,
        (shape(count, n), shape(count, n)),
        turn,
        (
            jnp.stack([sub.astype(jnp.int32), always, sub.astype(jnp.int32), choice.astype(jnp.int32)]),
            be_leaf, m_leaf, g_leaf, got_left, got_right, q_own, q_oth,
        ),
        "leaf_down",
    )
    received = swap(second)
    out = jnp.where(
        sub == 0,
        jnp.concatenate([first, received], axis=0),
        jnp.concatenate([received, first], axis=0),
    )
    return out[:, None, :]


def solution(mesh):
    placed = (
        P(("groups", "cols"), "leaf", "sub"),
        P(("groups", "leaf"), "sub", None),
        P(("groups", "leaf"), "sub", None),
        P(("groups", "leaf"), "sub", None),
        P(("groups", "leaf"), None, None),
        P(("groups", "leaf")),
    )
    return jax.shard_map(
        local,
        mesh=mesh,
        in_specs=placed,
        out_specs=P(("groups", "cols"), "leaf", "sub"),
        check_vma=False,
    )
```

```python
import functools

import jax
import jax.numpy as jnp
from jax import lax
from jax.experimental import pallas as pl
from jax.experimental.pallas import tpu as pltpu
from jax.sharding import PartitionSpec as P

f32 = jnp.float32
bf16 = jnp.bfloat16

VMEM_SPEC = pl.BlockSpec(memory_space=pltpu.VMEM)
SMEM_SPEC = pl.BlockSpec(memory_space=pltpu.SMEM)
NN = (((1,), (0,)), ((), ()))
NT = (((1,), (1,)), ((), ()))


def split(x):
    high = x.astype(bf16)
    return high, (x - high.astype(f32)).astype(bf16)


def one(a, b, dims=NN):
    return lax.dot_general(a, b, dims, preferred_element_type=f32)


def product(a, b, dims=NN):
    axis = dims[0][1][0]
    left = jnp.concatenate([a[0], a[1], a[0]], axis=1)
    return one(left, jnp.concatenate([b[0], b[0], b[1]], axis=axis), dims)


def eye(n):
    return (
        lax.broadcasted_iota(jnp.int32, (n, n), 0) == lax.broadcasted_iota(jnp.int32, (n, n), 1)
    ).astype(f32)


def invert(e_ref, x_ref, r_ref):
    n = e_ref.shape[0]
    e = e_ref[...]
    bound = jnp.max(jnp.sum(jnp.abs(e), axis=0, keepdims=True))
    scale = 1.9 / bound
    start = eye(n) - scale * e
    x_ref[...] = scale * (eye(n) + start)
    low = start.astype(bf16)
    first = one(low, low)
    r_ref[...] = first

    def rough_go(state):
        step, size = state
        return jnp.logical_and(step < 40, size > 4e-3)

    def rough(state):
        step, _ = state
        r = r_ref[...].astype(bf16)
        x = x_ref[...]
        both = one(jnp.concatenate([x.astype(bf16), r], axis=0), r)
        x_ref[...] = x + both[:n]
        squared = both[n:]
        r_ref[...] = squared
        return step + 1, jnp.sum(squared * squared)

    lax.while_loop(rough_go, rough, (jnp.int32(0), jnp.sum(first * first)))
    e_parts = split(e_ref[...])

    def residual():
        r = eye(n) - product(e_parts, split(x_ref[...]))
        r_ref[...] = r
        return jnp.sum(r * r)

    size = residual()
    restart = jnp.logical_not(size < 0.25)

    @pl.when(restart)
    def _():
        x_ref[...] = scale * eye(n)
        residual()

    def fine_go(state):
        step, now, before = state
        stalled = jnp.logical_and(before < 1e-2, now > 0.5 * before)
        more = jnp.logical_and(now > 1e-10, jnp.logical_not(stalled))
        return jnp.logical_and(step < 64, more)

    def fine(state):
        step, now, _ = state
        x = x_ref[...]
        small = now < 1e-6
        r = r_ref[...]

        @pl.when(now < 1e-2)
        def _():
            x_ref[...] = x + one(x.astype(bf16), r.astype(bf16))

        @pl.when(jnp.logical_not(now < 1e-2))
        def _():
            x_ref[...] = x + product(split(x), split(r))

        after = lax.cond(small, lambda: jnp.float32(0.0), residual)
        return step + 1, after, now

    lax.while_loop(
        fine_go, fine, (jnp.int32(0), jnp.where(restart, jnp.float32(1e6), size), jnp.float32(1e9))
    )


def wide_product(a, b, store):
    full = b[0].shape[1]
    width = 256 if full % 256 == 0 else full

    def block(j, carry):
        columns = pl.ds(pl.multiple_of(j * width, width), width)
        store(columns, product((a[0][...], a[1][...]), (b[0][:, columns], b[1][:, columns])))
        return carry

    lax.fori_loop(0, full // width, block, 0)


def eliminate(a, q, qt, b, p, t_ref, e_ref, m_ref, r_ref):
    n = e_ref.shape[0]

    def store_p(columns, value):
        p[0][:, columns], p[1][:, columns] = split(value)

    full_width = t_ref.shape[0]
    wide_product(a, q, store_p)
    width = full_width // 3
    for j in range(3):
        below, columns = slice(0, (j + 1) * width), slice(j * width, (j + 1) * width)
        t_ref[below, columns] = product(
            (qt[0][below, :], qt[1][below, :]), (p[0][:, columns], p[1][:, columns])
        )
    t_ref[width:n, :width] = t_ref[:width, width:n].T
    t_ref[2 * width :, n : 2 * width] = t_ref[n : 2 * width, 2 * width :].T
    e_ref[...] = t_ref[:n, :n]
    invert(e_ref, m_ref, r_ref)
    c = t_ref[:n, n:]
    g = product(split(m_ref[...]), split(c))
    g_parts = split(g)
    schur = t_ref[n:, n:] - product(split(c.T), g_parts)
    bq = product(b, (q[0][...], q[1][...]))
    be = bq[:, :n]
    carried = bq[:, n:] - product(split(be), g_parts)
    return schur, carried, g, be


def load_rotation(sub, q_own, q_oth, q, qt):
    n = q_own.shape[0]
    for which, ref in ((sub, q_own), (1 - sub, q_oth)):
        rows = pl.ds(pl.multiple_of(which * n, n), n)
        high, low = split(ref[...])
        q[0][rows, :] = high
        q[1][rows, :] = low
    if qt is not None:
        qt[0][...] = q[0][...].T
        qt[1][...] = q[1][...].T


def pack(sub, s_ref, c, out):
    n = s_ref.shape[0]
    b = n // 3

    @pl.when(sub == 0)
    def _():
        out[:n, :] = s_ref[:, :b]

    @pl.when(sub != 0)
    def _():
        out[: 2 * b, :] = s_ref[b:, b : 2 * b]
        out[2 * b : n, :] = s_ref[2 * b :, 2 * b :]

    count = c.shape[0]
    for j in range(3):
        out[n + j * count : n + (j + 1) * count, :] = c[:, j * b : (j + 1) * b]


def unpack(sub, own, oth):
    b = own.shape[1]
    n = 3 * b
    one_, two = by_half(sub, own[:n, :], oth[:n, :])
    top = jnp.concatenate([one_[:b], one_[b : 2 * b].T, one_[2 * b :].T], axis=1)
    mid = jnp.concatenate([one_[b : 2 * b], two[:b], two[b : 2 * b].T], axis=1)
    end = jnp.concatenate([one_[2 * b :], two[b : 2 * b], two[2 * b :]], axis=1)
    count = (own.shape[0] - n) // 3
    c = jnp.concatenate([own[n + j * count : n + (j + 1) * count, :] for j in range(3)], axis=1)
    return jnp.concatenate([top, mid, end], axis=0), c


def by_half(sub, own, oth):
    first = sub == 0
    return jnp.where(first, own, oth), jnp.where(first, oth, own)


def recover(be, m, g, x, q):
    w = product(split(be), split(m)) - product(split(x), split(g), NT)
    return product(split(jnp.concatenate([w, x], axis=1)), (q[0][...], q[1][...]), NT)


def leaf_kernel(
    flags, a_own, a_oth, q_own, q_oth, b_own, b_oth,
    s_out, load_out, c_out, m_out, g_out, be_out,
    ah, al, qh, ql, qth, qtl, ph, pl_, t_ref, e_ref, r_ref,
):
    sub = flags[0]
    load_rotation(sub, a_own, a_oth, (ah, al), None)
    load_rotation(sub, q_own, q_oth, (qh, ql), (qth, qtl))
    b = jnp.concatenate(by_half(sub, b_own[...], b_oth[...]), axis=1)
    s, c, g, be = eliminate(
        (ah, al), (qh, ql), (qth, qtl), split(b), (ph, pl_), t_ref, e_ref, m_out, r_ref
    )
    s_out[...] = s
    pack(sub, s_out, c, load_out)
    c_out[...] = c
    g_out[...] = g
    be_out[...] = be


def node_kernel(is_root, right_whole, *refs):
    flags, l_own, l_oth = refs[:3]
    refs = refs[3:]
    if right_whole:
        (r_whole, r_carried), refs = refs[:2], refs[2:]
    else:
        (r_own, r_oth), refs = refs[:2], refs[2:]
    (coup, q_own, q_oth), refs = refs[:3], refs[3:]
    if is_root:
        (left_out, right_out), refs = refs[:2], refs[2:]
        (x_ref, g_ref, s_ref, minv_ref), refs = refs[:4], refs[4:]
    else:
        (load_out, x_ref, g_ref, be_out), refs = refs[:4], refs[4:]
        (s_ref,), refs = refs[:1], refs[1:]
    ah, al, qh, ql, qth, qtl, ph, pl_, t_ref, e_ref, r_ref = refs
    sub = flags[0]
    n = e_ref.shape[0]

    @pl.when(flags[1] != 0)
    def _():
        load_rotation(sub, q_own, q_oth, (qh, ql), (qth, qtl))
        flipped = flags[2] != 0
        left, cl = unpack(sub, l_own, l_oth)
        if right_whole:
            right, cr = r_whole[...], r_carried[...]
        else:
            right, cr = unpack(sub, r_own, r_oth)
        coupling = coup[...]
        for row, col, value in (
            (0, 0, jnp.where(flipped, right, left)),
            (0, n, coupling),
            (n, 0, coupling.T),
            (n, n, jnp.where(flipped, left, right)),
        ):
            high, low = split(value)
            ah[row : row + n, col : col + n] = high
            al[row : row + n, col : col + n] = low
        b = jnp.concatenate(
            [jnp.where(flipped, cr, cl), jnp.where(flipped, cl, cr)], axis=1
        )
        s, c, g, be = eliminate(
            (ah, al), (qh, ql), (qth, qtl), split(b), (ph, pl_), t_ref, e_ref, x_ref, r_ref
        )
        s_ref[...] = s
        g_ref[...] = g
        if is_root:
            invert(s_ref, minv_ref, r_ref)
            x = product(split(c), split(minv_ref[...]))
            v = recover(be, x_ref[...], g_ref[...], x, (qh, ql))
            left_out[...] = jnp.where(flipped, v[:, n:], v[:, :n])
            right_out[...] = jnp.where(flipped, v[:, :n], v[:, n:])
        else:
            pack(sub, s_ref, c, load_out)
            be_out[...] = be


def down_kernel(flags, be, m, g, xa, xb, q_own, q_oth, left_out, right_out, qh, ql):
    sub = flags[0]
    n = m.shape[0]

    @pl.when(flags[1] != 0)
    def _():
        load_rotation(sub, q_own, q_oth, (qh, ql), None)
        x = jnp.where(flags[3] != 0, xa[...], xb[...])
        v = recover(be[...], m[...], g[...], x, (qh, ql))
        flipped = flags[2] != 0
        left_out[...] = jnp.where(flipped, v[:, n:], v[:, :n])
        right_out[...] = jnp.where(flipped, v[:, :n], v[:, n:])


def shape(*dims):
    return jax.ShapeDtypeStruct(dims, f32)


def call(kernel, outs, scratch, args, name):
    return pl.pallas_call(
        kernel,
        out_shape=outs,
        in_specs=[SMEM_SPEC] + [VMEM_SPEC] * (len(args) - 1),
        out_specs=jax.tree.map(lambda _: VMEM_SPEC, outs),
        scratch_shapes=scratch,
        compiler_params=pltpu.CompilerParams(vmem_limit_bytes=36 * 2**20),
        name=name,
    )(*args)


def swap(value):
    return lax.ppermute(value, "sub", [(0, 1), (1, 0)])


def hop(value, pairs):
    return lax.ppermute(value, "leaf", pairs)


def local(right_side, leaf_diag, leaf_rot, node_rot, coupling, child_order):
    sub = lax.axis_index("sub")
    pos = lax.axis_index("leaf")
    leaves = lax.axis_size("leaf")
    levels = leaves.bit_length() - 1
    full = leaf_diag.shape[-1]
    n = coupling.shape[-1]
    count = right_side.shape[0] // 2
    load = (n + 3 * count, n // 3)

    b_all = right_side[:, 0, :]
    b_own = lax.dynamic_slice_in_dim(b_all, sub * count, count, 0)
    b_oth = swap(lax.dynamic_slice_in_dim(b_all, (1 - sub) * count, count, 0))
    q_own, a_own, r_own = leaf_rot[0], leaf_diag[0], node_rot[0]
    q_oth, a_oth, r_oth = swap(q_own), swap(a_own), swap(r_own)
    flip = child_order[0]

    def flags(active, choice):
        return jnp.stack(
            [sub.astype(jnp.int32), active.astype(jnp.int32), flip, choice.astype(jnp.int32)]
        )

    always = jnp.ones((), jnp.int32)
    big = [pltpu.VMEM((full, full), bf16)] * 8
    small = [pltpu.VMEM((full, full), f32)] + [pltpu.VMEM((n, n), f32)] * 2
    schur, payload, carried, m_leaf, g_leaf, be_leaf = call(
        leaf_kernel,
        (shape(n, n), shape(*load), shape(count, n), shape(n, n), shape(n, n), shape(count, n)),
        big + small,
        (flags(always, always), a_own, a_oth, q_own, q_oth, b_own, b_oth),
        "leaf_up",
    )
    kept = {}
    for level in range(1, levels + 1):
        span = 2 ** (level - 1)
        gaps = range(span, leaves, 2 * span)
        owner = pos % (2 * span) == span
        step = max(span // 2, 1)
        to_right = [(g - step, g) for g in gaps]
        l_own = hop(payload, to_right)
        if level == 1:
            right = (schur, carried)
        else:
            to_left = [(g + step, g) for g in gaps]
            got = hop(payload, to_left)
            right = (got, swap(got))
        is_root = level == levels
        args = (flags(owner, always), l_own, swap(l_own), *right, coupling[0], r_own, r_oth)
        body = functools.partial(node_kernel, is_root, level == 1)
        if is_root:
            left_x, right_x = call(
                body, (shape(count, n), shape(count, n)),
                [pltpu.VMEM((n, n), f32)] * 4 + big + small, args, "root",
            )
        else:
            payload, m_node, g_node, be_node = call(
                body,
                (shape(*load), shape(n, n), shape(n, n), shape(count, n)),
                [pltpu.VMEM((n, n), f32)] + big + small, args, "node_up",
            )
            kept[level] = (be_node, m_node, g_node)
    turn = [pltpu.VMEM((full, full), bf16)] * 2
    for level in range(levels, 0, -1):
        span = 2 ** (level - 1)
        gaps = range(span, leaves, 2 * span)
        if level < levels:
            owner = pos % (2 * span) == span
            left_x, right_x = call(
                down_kernel,
                (shape(count, n), shape(count, n)),
                turn,
                (flags(owner, choice), *kept[level], got_left, got_right, r_own, r_oth),
                "node_down",
            )
        if level == 1:
            got_left = hop(left_x, [(g, g - 1) for g in gaps])
            got_right = right_x
            choice = pos % 2 == 0
        else:
            step = span // 2
            got_left = hop(left_x, [(g, g - step) for g in gaps])
            got_right = hop(right_x, [(g, g + step) for g in gaps])
            choice = pos // span % 2 == 0
    first, second = call(
        down_kernel,
        (shape(count, n), shape(count, n)),
        turn,
        (
            jnp.stack([sub.astype(jnp.int32), always, sub.astype(jnp.int32), choice.astype(jnp.int32)]),
            be_leaf, m_leaf, g_leaf, got_left, got_right, q_own, q_oth,
        ),
        "leaf_down",
    )
    received = swap(second)
    out = jnp.where(
        sub == 0,
        jnp.concatenate([first, received], axis=0),
        jnp.concatenate([received, first], axis=0),
    )
    return out[:, None, :]


def solution(mesh):
    placed = (
        P(("groups", "cols"), "leaf", "sub"),
        P(("groups", "leaf"), "sub", None),
        P(("groups", "leaf"), "sub", None),
        P(("groups", "leaf"), "sub", None),
        P(("groups", "leaf"), None, None),
        P(("groups", "leaf")),
    )
    return jax.shard_map(
        local,
        mesh=mesh,
        in_specs=placed,
        out_specs=P(("groups", "cols"), "leaf", "sub"),
        check_vma=False,
    )
```

```python
import functools

import jax
import jax.numpy as jnp
from jax import lax
from jax.experimental import pallas as pl
from jax.experimental.pallas import tpu as pltpu
from jax.sharding import PartitionSpec as P

f32 = jnp.float32
bf16 = jnp.bfloat16

VMEM_SPEC = pl.BlockSpec(memory_space=pltpu.VMEM)
SMEM_SPEC = pl.BlockSpec(memory_space=pltpu.SMEM)
NN = (((1,), (0,)), ((), ()))
NT = (((1,), (1,)), ((), ()))


def split(x):
    high = x.astype(bf16)
    return high, (x - high.astype(f32)).astype(bf16)


def one(a, b, dims=NN):
    return lax.dot_general(a, b, dims, preferred_element_type=f32)


def product(a, b, dims=NN):
    axis = dims[0][1][0]
    left = jnp.concatenate([a[0], a[1], a[0]], axis=1)
    return one(left, jnp.concatenate([b[0], b[0], b[1]], axis=axis), dims)


def eye(n):
    return (
        lax.broadcasted_iota(jnp.int32, (n, n), 0) == lax.broadcasted_iota(jnp.int32, (n, n), 1)
    ).astype(f32)


def invert(e_ref, x_ref, r_ref):
    n = e_ref.shape[0]
    e = e_ref[...]
    bound = jnp.max(jnp.sum(jnp.abs(e), axis=0, keepdims=True))
    scale = 1.9 / bound
    start = eye(n) - scale * e
    x_ref[...] = scale * (eye(n) + start)
    low = start.astype(bf16)
    first = one(low, low)
    r_ref[...] = first

    def rough_go(state):
        step, size = state
        return jnp.logical_and(step < 40, size > 4e-3)

    def rough(state):
        step, _ = state
        r = r_ref[...].astype(bf16)
        x = x_ref[...]
        both = one(jnp.concatenate([x.astype(bf16), r], axis=0), r)
        x_ref[...] = x + both[:n]
        squared = both[n:]
        r_ref[...] = squared
        return step + 1, jnp.sum(squared * squared)

    lax.while_loop(rough_go, rough, (jnp.int32(0), jnp.sum(first * first)))
    e_parts = split(e_ref[...])

    def residual():
        r = eye(n) - product(e_parts, split(x_ref[...]))
        r_ref[...] = r
        return jnp.sum(r * r)

    size = residual()
    restart = jnp.logical_not(size < 0.25)

    @pl.when(restart)
    def _():
        x_ref[...] = scale * eye(n)
        r_ref[...] = eye(n) - scale * e_ref[...]

    def fine_go(state):
        step, now, before = state
        stalled = jnp.logical_and(before < 1e-2, now > 0.5 * before)
        more = jnp.logical_and(now > 1e-10, jnp.logical_not(stalled))
        return jnp.logical_and(step < 64, more)

    def fine(state):
        step, now, _ = state
        x = x_ref[...]
        small = now < 1e-6
        r = r_ref[...]

        @pl.when(now < 1e-2)
        def _():
            x_ref[...] = x + one(x.astype(bf16), r.astype(bf16))

        @pl.when(jnp.logical_not(now < 1e-2))
        def _():
            x_ref[...] = x + product(split(x), split(r))

        after = lax.cond(small, lambda: jnp.float32(0.0), residual)
        return step + 1, after, now

    lax.while_loop(
        fine_go, fine, (jnp.int32(0), jnp.where(restart, jnp.float32(1e6), size), jnp.float32(1e9))
    )


def wide_product(a, b, store):
    full = b[0].shape[1]
    width = 256 if full % 256 == 0 else full

    def block(j, carry):
        columns = pl.ds(pl.multiple_of(j * width, width), width)
        store(columns, product((a[0][...], a[1][...]), (b[0][:, columns], b[1][:, columns])))
        return carry

    lax.fori_loop(0, full // width, block, 0)


def eliminate(a, q, qt, b, p, t_ref, e_ref, m_ref, r_ref):
    n = e_ref.shape[0]

    def store_p(columns, value):
        p[0][:, columns], p[1][:, columns] = split(value)

    full_width = t_ref.shape[0]
    wide_product(a, q, store_p)
    width = full_width // 3
    for j in range(3):
        below, columns = slice(0, (j + 1) * width), slice(j * width, (j + 1) * width)
        t_ref[below, columns] = product(
            (qt[0][below, :], qt[1][below, :]), (p[0][:, columns], p[1][:, columns])
        )
    t_ref[width:n, :width] = t_ref[:width, width:n].T
    t_ref[2 * width :, n : 2 * width] = t_ref[n : 2 * width, 2 * width :].T
    e_ref[...] = t_ref[:n, :n]
    invert(e_ref, m_ref, r_ref)
    c = t_ref[:n, n:]
    g = product(split(m_ref[...]), split(c))
    g_parts = split(g)
    schur = t_ref[n:, n:] - product(split(c.T), g_parts)
    bq = product(b, (q[0][...], q[1][...]))
    be = bq[:, :n]
    carried = bq[:, n:] - product(split(be), g_parts)
    return schur, carried, g, be


def load_rotation(sub, q_own, q_oth, q, qt):
    n = q_own.shape[0]
    for which, ref in ((sub, q_own), (1 - sub, q_oth)):
        rows = pl.ds(pl.multiple_of(which * n, n), n)
        high, low = split(ref[...])
        q[0][rows, :] = high
        q[1][rows, :] = low
    if qt is not None:
        qt[0][...] = q[0][...].T
        qt[1][...] = q[1][...].T


def pack(sub, s_ref, c, out):
    n = s_ref.shape[0]
    b = n // 3

    @pl.when(sub == 0)
    def _():
        out[:n, :] = s_ref[:, :b]

    @pl.when(sub != 0)
    def _():
        out[: 2 * b, :] = s_ref[b:, b : 2 * b]
        out[2 * b : n, :] = s_ref[2 * b :, 2 * b :]

    count = c.shape[0]
    for j in range(3):
        out[n + j * count : n + (j + 1) * count, :] = c[:, j * b : (j + 1) * b]


def unpack(sub, own, oth):
    b = own.shape[1]
    n = 3 * b
    one_, two = by_half(sub, own[:n, :], oth[:n, :])
    top = jnp.concatenate([one_[:b], one_[b : 2 * b].T, one_[2 * b :].T], axis=1)
    mid = jnp.concatenate([one_[b : 2 * b], two[:b], two[b : 2 * b].T], axis=1)
    end = jnp.concatenate([one_[2 * b :], two[b : 2 * b], two[2 * b :]], axis=1)
    count = (own.shape[0] - n) // 3
    c = jnp.concatenate([own[n + j * count : n + (j + 1) * count, :] for j in range(3)], axis=1)
    return jnp.concatenate([top, mid, end], axis=0), c


def by_half(sub, own, oth):
    first = sub == 0
    return jnp.where(first, own, oth), jnp.where(first, oth, own)


def recover(be, m, g, x, q):
    w = product(split(be), split(m)) - product(split(x), split(g), NT)
    return product(split(jnp.concatenate([w, x], axis=1)), (q[0][...], q[1][...]), NT)


def keep(kept, g, be):
    n = g.shape[0]
    kept[n : 2 * n, :] = g
    kept[2 * n :, :] = be


def leaf_kernel(
    flags, a_own, a_oth, q_own, q_oth, b_own, b_oth,
    s_out, load_out, c_out, kept_out,
    ah, al, qh, ql, qth, qtl, ph, pl_, t_ref, e_ref, r_ref,
):
    sub = flags[0]
    load_rotation(sub, a_own, a_oth, (ah, al), None)
    load_rotation(sub, q_own, q_oth, (qh, ql), (qth, qtl))
    b = jnp.concatenate(by_half(sub, b_own[...], b_oth[...]), axis=1)
    s, c, g, be = eliminate(
        (ah, al), (qh, ql), (qth, qtl), split(b), (ph, pl_), t_ref, e_ref, kept_out.at[: q_own.shape[0], :], r_ref
    )
    s_out[...] = s
    pack(sub, s_out, c, load_out)
    c_out[...] = c
    keep(kept_out, g, be)


def node_kernel(is_root, right_whole, *refs):
    flags, l_own, l_oth = refs[:3]
    refs = refs[3:]
    if right_whole:
        (r_whole, r_carried), refs = refs[:2], refs[2:]
    else:
        (r_own, r_oth), refs = refs[:2], refs[2:]
    (coup, q_own, q_oth), refs = refs[:3], refs[3:]
    if is_root:
        (left_out, right_out), refs = refs[:2], refs[2:]
        (x_ref, g_ref, s_ref, minv_ref), refs = refs[:4], refs[4:]
    else:
        (load_out, kept_out), refs = refs[:2], refs[2:]
        (s_ref,), refs = refs[:1], refs[1:]
    ah, al, qh, ql, qth, qtl, ph, pl_, t_ref, e_ref, r_ref = refs
    sub = flags[0]
    n = e_ref.shape[0]
    if not is_root:
        x_ref = kept_out.at[:n, :]

    @pl.when(flags[1] != 0)
    def _():
        load_rotation(sub, q_own, q_oth, (qh, ql), (qth, qtl))
        flipped = flags[2] != 0
        left, cl = unpack(sub, l_own, l_oth)
        if right_whole:
            right, cr = r_whole[...], r_carried[...]
        else:
            right, cr = unpack(sub, r_own, r_oth)
        coupling = coup[...]
        for row, col, value in (
            (0, 0, jnp.where(flipped, right, left)),
            (0, n, coupling),
            (n, 0, coupling.T),
            (n, n, jnp.where(flipped, left, right)),
        ):
            high, low = split(value)
            ah[row : row + n, col : col + n] = high
            al[row : row + n, col : col + n] = low
        b = jnp.concatenate(
            [jnp.where(flipped, cr, cl), jnp.where(flipped, cl, cr)], axis=1
        )
        s, c, g, be = eliminate(
            (ah, al), (qh, ql), (qth, qtl), split(b), (ph, pl_), t_ref, e_ref, x_ref, r_ref
        )
        s_ref[...] = s
        if is_root:
            g_ref[...] = g
            invert(s_ref, minv_ref, r_ref)
            x = product(split(c), split(minv_ref[...]))
            v = recover(be, x_ref[...], g_ref[...], x, (qh, ql))
            left_out[...] = jnp.where(flipped, v[:, n:], v[:, :n])
            right_out[...] = jnp.where(flipped, v[:, :n], v[:, n:])
        else:
            pack(sub, s_ref, c, load_out)
            keep(kept_out, g, be)


def down_kernel(flags, kept, xa, xb, q_own, q_oth, left_out, right_out, qh, ql):
    sub = flags[0]
    n = kept.shape[1]

    @pl.when(flags[1] != 0)
    def _():
        load_rotation(sub, q_own, q_oth, (qh, ql), None)
        x = jnp.where(flags[3] != 0, xa[...], xb[...])
        v = recover(kept[2 * n :, :], kept[:n, :], kept[n : 2 * n, :], x, (qh, ql))
        flipped = flags[2] != 0
        left_out[...] = jnp.where(flipped, v[:, n:], v[:, :n])
        right_out[...] = jnp.where(flipped, v[:, :n], v[:, n:])


def shape(*dims):
    return jax.ShapeDtypeStruct(dims, f32)


def call(kernel, outs, scratch, args, name):
    return pl.pallas_call(
        kernel,
        out_shape=outs,
        in_specs=[SMEM_SPEC] + [VMEM_SPEC] * (len(args) - 1),
        out_specs=jax.tree.map(lambda _: VMEM_SPEC, outs),
        scratch_shapes=scratch,
        compiler_params=pltpu.CompilerParams(vmem_limit_bytes=36 * 2**20),
        name=name,
    )(*args)


def swap(value):
    return lax.ppermute(value, "sub", [(0, 1), (1, 0)])


def hop(value, pairs):
    return lax.ppermute(value, "leaf", pairs)


def local(right_side, leaf_diag, leaf_rot, node_rot, coupling, child_order):
    sub = lax.axis_index("sub")
    pos = lax.axis_index("leaf")
    leaves = lax.axis_size("leaf")
    levels = leaves.bit_length() - 1
    full = leaf_diag.shape[-1]
    n = coupling.shape[-1]
    count = right_side.shape[0] // 2
    load = (n + 3 * count, n // 3)

    b_all = right_side[:, 0, :]
    b_own = lax.dynamic_slice_in_dim(b_all, sub * count, count, 0)
    b_oth = swap(lax.dynamic_slice_in_dim(b_all, (1 - sub) * count, count, 0))
    q_own, a_own, r_own = leaf_rot[0], leaf_diag[0], node_rot[0]
    q_oth, a_oth, r_oth = swap(q_own), swap(a_own), swap(r_own)
    flip = child_order[0]

    def flags(active, choice):
        return jnp.stack(
            [sub.astype(jnp.int32), active.astype(jnp.int32), flip, choice.astype(jnp.int32)]
        )

    always = jnp.ones((), jnp.int32)
    big = [pltpu.VMEM((full, full), bf16)] * 8
    small = [pltpu.VMEM((full, full), f32)] + [pltpu.VMEM((n, n), f32)] * 2
    schur, payload, carried, kept_leaf = call(
        leaf_kernel,
        (shape(n, n), shape(*load), shape(count, n), shape(2 * n + count, n)),
        big + small,
        (flags(always, always), a_own, a_oth, q_own, q_oth, b_own, b_oth),
        "leaf_up",
    )
    kept = {}
    for level in range(1, levels + 1):
        span = 2 ** (level - 1)
        gaps = range(span, leaves, 2 * span)
        owner = pos % (2 * span) == span
        step = max(span // 2, 1)
        to_right = [(g - step, g) for g in gaps]
        l_own = hop(payload, to_right)
        if level == 1:
            right = (schur, carried)
        else:
            to_left = [(g + step, g) for g in gaps]
            got = hop(payload, to_left)
            right = (got, swap(got))
        is_root = level == levels
        args = (flags(owner, always), l_own, swap(l_own), *right, coupling[0], r_own, r_oth)
        body = functools.partial(node_kernel, is_root, level == 1)
        if is_root:
            left_x, right_x = call(
                body, (shape(count, n), shape(count, n)),
                [pltpu.VMEM((n, n), f32)] * 4 + big + small, args, "root",
            )
        else:
            payload, kept[level] = call(
                body,
                (shape(*load), shape(2 * n + count, n)),
                [pltpu.VMEM((n, n), f32)] + big + small, args, "node_up",
            )
    turn = [pltpu.VMEM((full, full), bf16)] * 2
    for level in range(levels, 0, -1):
        span = 2 ** (level - 1)
        gaps = range(span, leaves, 2 * span)
        if level < levels:
            owner = pos % (2 * span) == span
            left_x, right_x = call(
                down_kernel,
                (shape(count, n), shape(count, n)),
                turn,
                (flags(owner, choice), kept[level], got_left, got_right, r_own, r_oth),
                "node_down",
            )
        if level == 1:
            got_left = hop(left_x, [(g, g - 1) for g in gaps])
            got_right = right_x
            choice = pos % 2 == 0
        else:
            step = span // 2
            got_left = hop(left_x, [(g, g - step) for g in gaps])
            got_right = hop(right_x, [(g, g + step) for g in gaps])
            choice = pos // span % 2 == 0
    first, second = call(
        down_kernel,
        (shape(count, n), shape(count, n)),
        turn,
        (
            jnp.stack([sub.astype(jnp.int32), always, sub.astype(jnp.int32), choice.astype(jnp.int32)]),
            kept_leaf, got_left, got_right, q_own, q_oth,
        ),
        "leaf_down",
    )
    received = swap(second)
    out = jnp.where(
        sub == 0,
        jnp.concatenate([first, received], axis=0),
        jnp.concatenate([received, first], axis=0),
    )
    return out[:, None, :]


def solution(mesh):
    placed = (
        P(("groups", "cols"), "leaf", "sub"),
        P(("groups", "leaf"), "sub", None),
        P(("groups", "leaf"), "sub", None),
        P(("groups", "leaf"), "sub", None),
        P(("groups", "leaf"), None, None),
        P(("groups", "leaf")),
    )
    return jax.shard_map(
        local,
        mesh=mesh,
        in_specs=placed,
        out_specs=P(("groups", "cols"), "leaf", "sub"),
        check_vma=False,
    )
```
